128 devices in a mesh: dp: 8 (over y, core), expert: 16 (over x, z).
Axes of the slice: x: 4, y: 4, z: 4, core: 2. Of those that a mesh axis runs over, the one named last changes fastest.
Arguments:
- tokens: bfloat16 [16384, 4096], P(('dp', 'expert')), may hold values from -6 to 6
- expert_ids: int32 [16384, 2], P(('dp', 'expert')), may hold values from 0 to 63, all different within a row; in each aligned block of 128 rows (0 to 127, 128 to 255, ...) at most 6 rows name the same one
- gate_num: int32 [16384, 2], P(('dp', 'expert')), may hold values from 1 to 255
- out_grad: bfloat16 [16384, 4096], P(('dp', 'expert')), may hold values from -6 to 6
- gate_weight: bfloat16 [128, 4096, 384], P(('dp', 'expert')), may hold values from -0.09375 to 0.09375
- up_weight: bfloat16 [128, 4096, 384], P(('dp', 'expert')), may hold values from -0.09375 to 0.09375
- down_weight: bfloat16 [128, 384, 4096], P(('dp', 'expert')), may hold values from -0.21875 to 0.21875
Outputs:
- moe_out: bfloat16 [16384, 4096], P(('dp', 'expert'))
- token_grad: bfloat16 [16384, 4096], P(('dp', 'expert'))
- gate_grad: bfloat16 [128, 4096, 384], P(('dp', 'expert'))
- up_grad: bfloat16 [128, 4096, 384], P(('dp', 'expert'))
- down_grad: bfloat16 [128, 384, 4096], P(('dp', 'expert'))
The draws below stay inside these ranges and needn't reach their ends.
Inputs may be any that keep to these rules, and one draw needn't show every extreme that they name: `expert_ids`: each token names 2 different experts; among the 128 tokens of one device no expert is named by more than 6 routes, a bound that some block reaches. A route's gate weight is gate_num / 256.
All inputs are finite; a program needn't handle non-finite values.
Results may differ from the reference program's by a relative error of at most 0.0065.
Values may be sent and summed in bfloat16 or wider, within the bound.
A program may use at most 256 MiB of HBM per device.

```python
import math
import jax
import jax.numpy as jnp
import numpy as np
from jax import lax

D = 4096
FF = 768
TOP = 2
DEN = 256
TOK_DEV = 128
HALF = 384
EXPERTS = 64
CAP = 6
TOKENS = 16384
N_DP = 8
N_EXPERT = 16
DEVICES = 128


def touch_ends(values, key, smallest, high):
    dims = values.shape
    spot = [jax.random.randint(jax.random.fold_in(key, axis), (), 0, dims[axis]) for axis in range(len(dims))]
    values = values.at[tuple(spot)].set(smallest)
    longest = dims.index(max(dims))
    spot[longest] = (spot[longest] + 1) % dims[longest]
    return values.at[tuple(spot)].set(high)


def block_scale(own_key, extent, split, least, largest):
    def one(dim, parts):
        steps = jax.random.uniform(jax.random.fold_in(jax.random.fold_in(own_key, 6), dim), (parts,), jnp.float32, least / len(split), largest / len(split))
        return jnp.repeat(jnp.exp(steps), extent[dim] // parts).reshape((-1,) + (1,) * (len(extent) - dim - 1))

    level = one(*split[0])
    for cut in split[1:]:
        level = level * one(*cut)
    return level


def shared_out(key, own, number, rows, amount, top, most, slope):
    order = jax.random.permutation(key, amount)
    crowded, common = shares(amount, rows * top, most, slope, True), shares(amount, rows * top, most, slope, False)
    places = jnp.arange(amount)

    def named(sizes, offset_by):
        used = int((sizes > 0).sum())
        fixed = max(1, used // 4)
        moved = fixed + (places - fixed + offset_by * (used - fixed)) % max(1, amount - fixed)
        return jnp.zeros((amount,), jnp.int32).at[order[jnp.where(places < fixed, places, moved)]].set(jnp.asarray(sizes, jnp.int32))

    sizes = jnp.where(number % 4 == 0, named(crowded, number // 4), named(common, number - number // 4 - 1))
    mixed = jax.random.permutation(jax.random.fold_in(own, 3), amount)
    giver, sink = mixed[0:amount // 2 * 2:2], mixed[1:amount // 2 * 2:2]
    margin = jnp.minimum(sizes[giver] - 1, most - sizes[sink]) // 2
    margin = jnp.where((giver == order[0]) | (sink == order[0]) | (sizes[sink] == 0), 0, jnp.maximum(margin, 0))
    moved = jax.random.randint(jax.random.fold_in(own, 4), (amount // 2,), 0, 1 << 20) % (margin + 1)
    sizes = sizes.at[giver].add(-moved).at[sink].add(moved)
    labels = jnp.searchsorted(jnp.cumsum(sizes), jnp.arange(rows * top), side="right").astype(jnp.int32)
    listing = labels.reshape(top, rows).T
    listing = listing[jax.random.permutation(jax.random.fold_in(own, 1), rows)]
    offset_by = jax.random.randint(jax.random.fold_in(own, 2), (rows, 1), 0, top)
    return jnp.take_along_axis(listing, (jnp.arange(top)[None, :] + offset_by) % top, axis=1)


def shares(amount, total, reach, slope, full):
    portions = [(1 << 20) // math.isqrt(grade ** slope) + 1 for grade in range(1, amount + 1)]
    largest = reach if full else min(reach, max(-(-total // amount), total * portions[0] // sum(portions)))
    least = 1 if total - largest >= amount - 1 else 0
    counts, rest = [largest] + [least] * (amount - 1), total - largest - least * (amount - 1)
    while rest > 0:
        candidates = [i for i in range(1, amount) if counts[i] < largest] or [i for i in range(1, amount) if counts[i] < reach]
        mass, left = sum([portions[i] for i in candidates]), rest
        for i in candidates:
            addition = min(reach - counts[i], max(1, left * portions[i] // mass), rest)
            counts[i] = counts[i] + addition
            rest = rest - addition
    return np.array(counts)


def normal_values(rng, shape, scale, most, split=(), kind=jnp.bfloat16):
    array = jax.random.normal(rng, shape, jnp.float32) * scale
    if len(split) > 0:
        array = block_scale(rng, shape, split, -0.22, 0.18) * array
    return jnp.clip(array, min=-most, max=most).astype(kind)


def setup_inputs(seed: int = 0) -> dict:
    seeds = jax.random.split(jax.random.key(seed), 8)
    tokens = normal_values(seeds[0], (TOKENS, D), 1.0, 6.0, ((0, 128),))
    expert_ids_keys = jax.random.split(jax.random.fold_in(seeds[1], 1), TOKENS // TOK_DEV)
    expert_ids_turns = jax.random.permutation(jax.random.fold_in(seeds[1], 3), TOKENS // TOK_DEV)
    expert_ids = jax.vmap(lambda own, number: shared_out(jax.random.fold_in(seeds[1], 2), own, number, TOK_DEV, EXPERTS, TOP, CAP, 2))(expert_ids_keys, expert_ids_turns).reshape((TOKENS, TOP))
    gate_num = touch_ends(jax.random.randint(seeds[2], (TOKENS, TOP), 1, 256), jax.random.fold_in(seeds[2], 1), 1, 255).astype(jnp.int32)
    out_grad = normal_values(seeds[3], (TOKENS, D), 1.0, 6.0, ((0, 128),))
    gate_weight = normal_values(seeds[4], (DEVICES, D, HALF), D ** -0.5, 0.09375, ((0, 128),))
    up_weight = normal_values(seeds[5], (DEVICES, D, HALF), D ** -0.5, 0.09375, ((0, 128),))
    down_weight = normal_values(seeds[6], (DEVICES, HALF, D), FF ** -0.5, 0.21875, ((0, 128),))
    return {"tokens": tokens, "expert_ids": expert_ids, "gate_num": gate_num, "out_grad": out_grad, "gate_weight": gate_weight, "up_weight": up_weight, "down_weight": down_weight}


def reference(tokens, expert_ids, gate_num, out_grad, gate_weight, up_weight, down_weight):
    device_count = N_DP * N_EXPERT
    routes_dev = TOK_DEV * TOP
    grouped = expert_ids.reshape(device_count, routes_dev)
    onehot = (grouped[:, :, None] == jnp.arange(EXPERTS, dtype=jnp.int32)[None, None, :]).astype(jnp.int32)
    before = jnp.cumsum(onehot, axis=1) - onehot
    route_rank = jnp.sum(before * onehot, axis=2)
    source = jnp.arange(device_count, dtype=jnp.int32)[:, None]
    slot_row = (source * CAP + route_rank).reshape(-1).astype(jnp.int32)
    route_expert = expert_ids.reshape(-1).astype(jnp.int32)
    route_token = (jnp.arange(TOKENS * TOP, dtype=jnp.int32) // TOP).astype(jnp.int32)
    gate_values = gate_num.reshape(-1).astype(jnp.float32) / DEN
    row_total = device_count * CAP
    dispatched = jnp.zeros((EXPERTS, row_total, D), jnp.bfloat16).at[route_expert, slot_row].set(tokens[route_token])
    scaled = (gate_values[:, None] * out_grad[route_token].astype(jnp.float32)).astype(jnp.bfloat16)
    routed_grad = jnp.zeros((EXPERTS, row_total, D), jnp.bfloat16).at[route_expert, slot_row].set(scaled)

    def one_expert(packed):
        expert_idx, rows_x, rows_g = packed
        gate_full = jnp.concatenate([gate_weight[expert_idx], gate_weight[expert_idx + EXPERTS]], axis=1)
        up_full = jnp.concatenate([up_weight[expert_idx], up_weight[expert_idx + EXPERTS]], axis=1)
        down_full = jnp.concatenate([down_weight[expert_idx], down_weight[expert_idx + EXPERTS]], axis=0)
        gate_act = jnp.dot(rows_x, gate_full, preferred_element_type=jnp.float32)
        up_act = jnp.dot(rows_x, up_full, preferred_element_type=jnp.float32)
        sigmoid_gate = jax.nn.sigmoid(gate_act)
        silu_gate = gate_act * sigmoid_gate
        hidden = (silu_gate * up_act).astype(jnp.bfloat16)
        expert_out = jnp.dot(hidden, down_full, preferred_element_type=jnp.float32).astype(jnp.bfloat16)
        hidden_grad = jnp.dot(rows_g, down_full.T, preferred_element_type=jnp.float32)
        down_grad = jnp.dot(hidden.T, rows_g, preferred_element_type=jnp.float32).astype(jnp.bfloat16)
        up_grad_act = (hidden_grad * silu_gate).astype(jnp.bfloat16)
        gate_grad_act = (hidden_grad * up_act * sigmoid_gate * (1.0 + gate_act * (1.0 - sigmoid_gate))).astype(jnp.bfloat16)
        gate_grad = jnp.dot(rows_x.T, gate_grad_act, preferred_element_type=jnp.float32).astype(jnp.bfloat16)
        up_grad = jnp.dot(rows_x.T, up_grad_act, preferred_element_type=jnp.float32).astype(jnp.bfloat16)
        row_grad = jnp.dot(gate_grad_act, gate_full.T, preferred_element_type=jnp.float32)
        row_grad = (row_grad + jnp.dot(up_grad_act, up_full.T, preferred_element_type=jnp.float32)).astype(jnp.bfloat16)
        return expert_out, row_grad, gate_grad, up_grad, down_grad

    expert_out, row_grad, gate_grad, up_grad, down_grad = lax.map(
        one_expert, (jnp.arange(EXPERTS, dtype=jnp.int32), dispatched, routed_grad))
    picked_out = expert_out[route_expert, slot_row].astype(jnp.float32) * gate_values[:, None]
    moe_out = jnp.sum(picked_out.reshape(TOKENS, TOP, D), axis=1).astype(jnp.bfloat16)
    picked_grad = row_grad[route_expert, slot_row].astype(jnp.float32)
    token_grad = jnp.sum(picked_grad.reshape(TOKENS, TOP, D), axis=1).astype(jnp.bfloat16)
    gate_blocks = jnp.concatenate([gate_grad[:, :, :HALF], gate_grad[:, :, HALF:]], axis=0)
    up_blocks = jnp.concatenate([up_grad[:, :, :HALF], up_grad[:, :, HALF:]], axis=0)
    down_blocks = jnp.concatenate([down_grad[:, :HALF, :], down_grad[:, HALF:, :]], axis=0)
    return (moe_out, token_grad, gate_blocks, up_blocks, down_blocks)
```

```python
import jax
import jax.numpy as jnp
from jax import lax
from jax.sharding import PartitionSpec as P

DEN = 256


def route_slots(expert_ids, gate_num, expert_count, capacity):
    tok_rows, route_count = expert_ids.shape
    routes = tok_rows * route_count
    flat_ids = expert_ids.reshape(-1)
    onehot = flat_ids[:, None] == jnp.arange(expert_count, dtype=jnp.int32)[None, :]
    order = jnp.arange(routes, dtype=jnp.int32)
    earlier = (order[None, :] < order[:, None]).astype(jnp.bfloat16)
    before = jnp.dot(earlier, onehot.astype(jnp.bfloat16), preferred_element_type=jnp.float32)
    route_rank = jnp.sum(jnp.where(onehot, before, 0.0), axis=1).astype(jnp.int32)
    slot = (flat_ids * capacity + route_rank).reshape(tok_rows, route_count)
    gate_values = gate_num.astype(jnp.float32) / DEN
    rows = jnp.arange(expert_count * capacity, dtype=jnp.int32)[:, None]
    hits = [rows == slot[None, :, k] for k in range(route_count)]
    placer = sum(h.astype(jnp.float32) for h in hits)
    weigher = sum(jnp.where(h, gate_values[None, :, k], 0.0) for k, h in enumerate(hits))
    return placer.astype(jnp.bfloat16), weigher.astype(jnp.bfloat16)


def exchange(rows, device_count, capacity):
    width = rows.shape[-1]
    blocks = rows.reshape(device_count, capacity * 4, width // 4)
    got = lax.all_to_all(blocks, ("dp", "expert"), split_axis=0, concat_axis=0, tiled=True)
    return got.reshape(device_count * capacity, width)


def on_device(tokens, expert_ids, gate_num, out_grad, gate_weight, up_weight, down_weight):
    device_count = lax.axis_size("dp") * lax.axis_size("expert")
    expert_count = device_count // 2
    tok_rows, route_count = expert_ids.shape
    capacity = 2 * ((3 * tok_rows * route_count + 4 * expert_count - 1) // (4 * expert_count))
    placer, weigher = route_slots(expert_ids, gate_num, expert_count, capacity)
    bf16, f32 = jnp.bfloat16, jnp.float32
    placer2 = jnp.concatenate([placer, placer], axis=0)
    weigher2 = jnp.concatenate([weigher, weigher], axis=0)
    x_rows = jnp.dot(placer2, tokens, preferred_element_type=f32).astype(bf16)
    g_rows = jnp.dot(weigher2, out_grad, preferred_element_type=f32).astype(bf16)
    rows_in = exchange(x_rows, device_count, capacity)
    grads_in = exchange(g_rows, device_count, capacity)
    gate_block, up_block, down_block = gate_weight[0], up_weight[0], down_weight[0]
    gate_act = jnp.dot(rows_in, gate_block, preferred_element_type=f32)
    up_act = jnp.dot(rows_in, up_block, preferred_element_type=f32)
    sigmoid_gate = jax.nn.sigmoid(gate_act)
    silu_gate = gate_act * sigmoid_gate
    hidden = (silu_gate * up_act).astype(bf16)
    partial_out = jnp.dot(hidden, down_block, preferred_element_type=f32).astype(bf16)
    out_back = exchange(partial_out, device_count, capacity)
    last = (((1,), (1,)), ((), ()))
    first = (((0,), (0,)), ((), ()))
    hidden_grad = lax.dot_general(grads_in, down_block, last, preferred_element_type=f32)
    up_grad_act = (hidden_grad * silu_gate).astype(bf16)
    gate_grad_act = (
        hidden_grad * up_act * sigmoid_gate * (1.0 + gate_act * (1.0 - sigmoid_gate))
    ).astype(bf16)
    row_part = lax.dot_general(gate_grad_act, gate_block, last, preferred_element_type=f32)
    row_part = row_part + lax.dot_general(
        up_grad_act, up_block, last, preferred_element_type=f32
    )
    row_back = exchange(row_part.astype(bf16), device_count, capacity)
    down_grad = lax.dot_general(hidden, grads_in, first, preferred_element_type=f32)
    gate_grad = lax.dot_general(rows_in, gate_grad_act, first, preferred_element_type=f32)
    up_grad = lax.dot_general(rows_in, up_grad_act, first, preferred_element_type=f32)
    moe_out = lax.dot_general(weigher2, out_back, first, preferred_element_type=f32)
    token_grad = lax.dot_general(placer2, row_back, first, preferred_element_type=f32)
    return (
        moe_out.astype(bf16),
        token_grad.astype(bf16),
        gate_grad.astype(bf16)[None],
        up_grad.astype(bf16)[None],
        down_grad.astype(bf16)[None],
    )


def solution(mesh):
    rows = P(("dp", "expert"), None)
    blocks = P(("dp", "expert"), None, None)
    return jax.shard_map(
        on_device,
        mesh=mesh,
        in_specs=(rows, rows, rows, rows, blocks, blocks, blocks),
        out_specs=(rows, rows, blocks, blocks, blocks),
        check_vma=False,
    )
```

```python
import jax
import jax.numpy as jnp
from jax import lax
from jax.experimental import pallas as pl
from jax.experimental.pallas import tpu as pltpu
from jax.sharding import PartitionSpec as P

DEN = 256
MESH = pl.DeviceIdType.MESH
BF16, F32 = jnp.bfloat16, jnp.float32
CHUNKS = 2
PLANE = ((0, 1), (1, 0), (0, 3), (3, 0), (2, 2), (1, 1), (3, 3), (1, 3), (3, 1), (0, 2), (2, 0),
         (1, 2), (3, 2), (2, 1), (2, 3))
DPS = ((1, 0), (3, 0), (2, 0), (1, 1), (3, 1), (2, 1), (0, 1))


def place():
    dp, ex = lax.axis_index("dp"), lax.axis_index("expert")
    return dp // 2, dp % 2, ex // 4, ex % 4


def span(start, size):
    return pl.ds(pl.multiple_of(start, 16), size)


def remote(src, dst, s, r, yy, cc, xx, zz):
    return pltpu.make_async_remote_copy(
        src_ref=src, dst_ref=dst, send_sem=s, recv_sem=r,
        device_id=(yy * 2 + cc, xx * 4 + zz), device_id_type=MESH)


def dispatch(xs, og, wts, pi, spread, x_out, g_out, wbig, a1r, a2s, ogr, wr, b2s, a1_s, a1_r,
             b1_s, b1_r, sb_s, sb_r, w_s, w_r, a2_s, a2_r, b2_s, b2_r, l_s):
    y, c, x, z = place()
    dp, ex = y * 2 + c, x * 4 + z
    half = og.shape[1] // 2
    fold = half // CHUNKS
    wide = og.shape[1] // CHUNKS
    me = c * 4 + y
    own = [
        pltpu.make_async_copy(xs.at[span(ex * 48, 48)], a1r.at[span(ex * 48, 48)], l_s.at[0]),
        pltpu.make_async_copy(og, ogr.at[span(me * 128, 128)], l_s.at[1]),
        pltpu.make_async_copy(wts.at[span(dp % 4 * 96, 96)], wr.at[me], l_s.at[2]),
    ]
    for o in own:
        o.start()
    w_cp = []
    for d, dc in DPS:
        yy, cc = (y + d) % 4, (c + dc) % 2
        w_cp.append(remote(wts.at[span((yy * 2 + cc) % 4 * 96, 96)], wr.at[me],
                           w_s.at[d * 2 + dc], w_r.at[d * 2 + dc], yy, cc, x, z))
        w_cp[-1].start()
    a1, b1, sb, a2, b2, last = [], [], [], [], [], []
    for k in range(CHUNKS):
        thin, cols = pl.ds(k * fold, fold), pl.ds(k * wide, wide)
        b1.append([remote(og.at[:, cols], ogr.at[span(me * 128, 128), cols],
                          b1_s.at[k, d], b1_r.at[k, d], (y + d) % 4, c, x, z) for d in (1, 3, 2)])
        sb.append([remote(og.at[:, cols], ogr.at[span(me * 128, 128), cols],
                          sb_s.at[k, 0], sb_r.at[k, 0], y, 1 - c, x, z)])
        a1.append([])
        for dx, dz in PLANE:
            xx, zz = (x + dx) % 4, (z + dz) % 4
            a1[k].append(remote(
                xs.at[span((xx * 4 + zz) * 48, 48), thin], a1r.at[span(ex * 48, 48), thin],
                a1_s.at[k, dx * 4 + dz], a1_r.at[k, dx * 4 + dz], y, c, xx, zz))
        for cp in b1[k] + sb[k] + a1[k]:
            cp.start()
    for o in own:
        o.wait()
    for w in w_cp:
        w.wait_recv()
    for s in range(8):
        wbig[:, s * 128:(s + 1) * 128] = jnp.dot(
            spread[s], wr[s], preferred_element_type=F32).astype(BF16)
    for k in range(CHUNKS):
        thin, cols = pl.ds(k * fold, fold), pl.ds(k * wide, wide)
        for d, cp in zip((1, 3, 2), b1[k]):
            cp.wait_recv()
            block = ogr.at[span((c * 4 + (y + 4 - d) % 4) * 128, 128), cols]
            sb[k].append(remote(block, block, sb_s.at[k, d], sb_r.at[k, d], y, 1 - c, x, z))
            sb[k][-1].start()
        for cp in a1[k]:
            cp.wait_recv()
        a2.append([])
        for dy in (1, 0):
            for dc in (0, 1):
                cc = (c + dc) % 2
                q = ((y + dy) % 2) * 2 + cc
                for h in range(2):
                    part = pl.ds(h * half + k * fold, fold)
                    a2s[span(q * 96, 96), part] = jnp.dot(
                        pi[span((q * 2 + h) * 96, 96), :], a1r[:, thin],
                        preferred_element_type=F32).astype(BF16)
                    for far in (0, 2):
                        d = dy + far
                        spot = x_out.at[span(dp * 96, 96), part]
                        if d == 0 and dc == 0:
                            cp = pltpu.make_async_copy(
                                a2s.at[span(q * 96, 96), part], spot, l_s.at[3 + k * 2 + h])
                            last.append(cp)
                        else:
                            n = (d * 2 + dc) * 2 + h
                            cp = remote(a2s.at[span(q * 96, 96), part], spot, a2_s.at[k, n],
                                        a2_r.at[k, n], (y + d) % 4, cc, x, z)
                            a2[k].append(cp)
                        cp.start()
        for cp in sb[k]:
            cp.wait_recv()
        for h in range(4):
            band = pl.ds(h * 192, 192)
            b2s[band, cols] = jnp.dot(
                wbig[band, :], ogr[:, cols], preferred_element_type=F32).astype(BF16)
        b2.append([])
        spot = g_out.at[span(ex * 48, 48), cols]
        for dx, dz in PLANE:
            xx, zz = (x + dx) % 4, (z + dz) % 4
            n = dx * 4 + dz
            b2[k].append(remote(b2s.at[span((xx * 4 + zz) * 48, 48), cols], spot,
                                b2_s.at[k, n], b2_r.at[k, n], y, c, xx, zz))
            b2[k][-1].start()
        last.append(pltpu.make_async_copy(b2s.at[span(ex * 48, 48), cols], spot, l_s.at[7 + k]))
        last[-1].start()
    for k in range(CHUNKS):
        for cp in a2[k] + b2[k]:
            cp.wait_recv()
    for cp in last:
        cp.wait()
    for cp in w_cp + sum(a1 + b1 + sb + a2 + b2, []):
        cp.wait_send()


def homeward(out_b, row_a, wbig_t, pi_t, placer_t, moe, tok, br, ar, tot, part, sibr, partr, back,
             backr, c1_s, c1_r, d1_s, d1_r, sb_s, sb_r, c2_s, c2_r, d2_s, d2_r, l_s):
    y, c, x, z = place()
    dp, ex = y * 2 + c, x * 4 + z
    half = out_b.shape[1] // 2
    fold = half // CHUNKS
    wide = out_b.shape[1] // CHUNKS
    c1, d1, sb, c2, d2, own1, own2 = [], [], [], [], [], [], []
    for k in range(CHUNKS):
        cols = pl.ds(k * wide, wide)
        own1.append([pltpu.make_async_copy(
            out_b.at[span(ex * 48, 48), cols], br.at[span(ex * 48, 48), cols], l_s.at[k])])
        d1.append([])
        for h in range(2):
            piece = pl.ds(h * half + k * fold, fold)
            own1[k].append(pltpu.make_async_copy(
                row_a.at[span(dp * 96, 96), piece], ar.at[span(dp * 96, 96), piece],
                l_s.at[2 + k * 2 + h]))
            for d, dc in DPS:
                yy, cc = (y + d) % 4, (c + dc) % 2
                n = (d * 2 + dc) * 2 + h
                d1[k].append(remote(
                    row_a.at[span((yy * 2 + cc) * 96, 96), piece],
                    ar.at[span(dp * 96, 96), piece], d1_s.at[k, n], d1_r.at[k, n], yy, cc, x, z))
        c1.append([])
        for dx, dz in PLANE:
            xx, zz = (x + dx) % 4, (z + dz) % 4
            n = dx * 4 + dz
            c1[k].append(remote(
                out_b.at[span((xx * 4 + zz) * 48, 48), cols], br.at[span(ex * 48, 48), cols],
                c1_s.at[k, n], c1_r.at[k, n], y, c, xx, zz))
        for cp in own1[k] + d1[k] + c1[k]:
            cp.start()
    for k in range(CHUNKS):
        thin, cols = pl.ds(k * fold, fold), pl.ds(k * wide, wide)
        for cp in own1[k]:
            cp.wait()
        for cp in c1[k]:
            cp.wait_recv()
        for s in range(4):
            band = pl.ds(s * 256, 256)
            part[band, cols] = jnp.dot(
                wbig_t[band, :], br[:, cols], preferred_element_type=F32).astype(BF16)
        sb.append(remote(part.at[span((1 - c) * 512, 512), cols], sibr.at[:, cols],
                         sb_s.at[k], sb_r.at[k], y, 1 - c, x, z))
        sb[k].start()
        for cp in d1[k]:
            cp.wait_recv()
        for q in range(4):
            for h in range(2):
                piece = pl.ds(h * half + k * fold, fold)
                tot[(q * 2 + h) * 96:(q * 2 + h + 1) * 96, :] = (
                    ar[q * 96:(q + 1) * 96, piece].astype(F32)
                    + ar[384 + q * 96:384 + (q + 1) * 96, piece].astype(F32)).astype(BF16)
        for h in range(4):
            band = pl.ds(h * 192, 192)
            back[band, thin] = jnp.dot(
                pi_t[band, :], tot[...], preferred_element_type=F32).astype(BF16)
        d2.append([])
        for dx, dz in PLANE:
            xx, zz = (x + dx) % 4, (z + dz) % 4
            n = dx * 4 + dz
            d2[k].append(remote(
                back.at[span((xx * 4 + zz) * 48, 48), thin], backr.at[span(ex * 48, 48), thin],
                d2_s.at[k, n], d2_r.at[k, n], y, c, xx, zz))
        own2.append([pltpu.make_async_copy(
            back.at[span(ex * 48, 48), thin], backr.at[span(ex * 48, 48), thin], l_s.at[6 + k])])
        for cp in d2[k] + own2[k]:
            cp.start()
        sb[k].wait_recv()
        sibr[:, cols] = (part[span(c * 512, 512), cols].astype(F32)
                         + sibr[:, cols].astype(F32)).astype(BF16)
        c2.append([])
        spot = partr.at[span(y * 128, 128), cols]
        for d in (1, 3, 2):
            yy = (y + d) % 4
            c2[k].append(remote(sibr.at[span(yy * 128, 128), cols], spot,
                                c2_s.at[k, d], c2_r.at[k, d], yy, c, x, z))
            c2[k][-1].start()
        own2[k].append(pltpu.make_async_copy(sibr.at[span(y * 128, 128), cols], spot,
                                             l_s.at[8 + k]))
        own2[k][-1].start()
    for k in range(CHUNKS):
        thin, cols = pl.ds(k * fold, fold), pl.ds(k * wide, wide)
        for cp in own2[k]:
            cp.wait()
        for cp in c2[k] + d2[k]:
            cp.wait_recv()
        for h in range(2):
            tok[:, pl.ds(h * half + k * fold, fold)] = jnp.dot(
                placer_t[h], backr[:, thin], preferred_element_type=F32).astype(BF16)
        moe[:, cols] = sum(
            partr[s * 128:(s + 1) * 128, cols].astype(F32) for s in range(4)).astype(BF16)
    for cp in sum(c1 + d1 + c2 + d2, sb):
        cp.wait_send()


VM = pl.BlockSpec(memory_space=pltpu.VMEM)
HB = pl.BlockSpec(memory_space=pltpu.HBM)


def sems(*sizes):
    return [pltpu.SemaphoreType.DMA(s) for s in sizes for _ in (0, 1)]


def vm(*shape):
    return pltpu.VMEM(shape, BF16)


def out(*shape):
    return jax.ShapeDtypeStruct(shape, BF16)


def call_dispatch(xs, og, wts, pi, spread):
    w, k = og.shape[1], CHUNKS
    return pl.pallas_call(
        dispatch,
        out_shape=(out(768, w), out(768, w), out(768, 1024)),
        in_specs=[VM] * 5,
        out_specs=(HB, HB, VM),
        scratch_shapes=[
            vm(768, w // 2), vm(384, w), vm(1024, w), vm(8, 96, 128), vm(768, w),
            *sems((k, 16), (k, 4), (k, 4), (8,), (k, 16), (k, 16)),
            pltpu.SemaphoreType.DMA((9,))],
        compiler_params=pltpu.CompilerParams(has_side_effects=True, vmem_limit_bytes=56 << 20),
    )(xs, og, wts, pi, spread)


def call_homeward(out_b, row_a, wbig_t, pi_t, placer_t):
    w, k = out_b.shape[1], CHUNKS
    return pl.pallas_call(
        homeward,
        out_shape=(out(128, w), out(128, w)),
        in_specs=[HB, HB, VM, VM, VM],
        out_specs=(VM, VM),
        scratch_shapes=[
            vm(768, w), vm(768, w), vm(768, w // 2 // k), vm(1024, w), vm(512, w), vm(512, w),
            vm(768, w // 2), vm(768, w // 2),
            *sems((k, 16), (k, 16), (k,), (k, 4), (k, 16)), pltpu.SemaphoreType.DMA((10,))],
        compiler_params=pltpu.CompilerParams(has_side_effects=True, vmem_limit_bytes=58 << 20),
    )(out_b, row_a, wbig_t, pi_t, placer_t)


def one_hot(index, size):
    return (index[:, None] == jnp.arange(size, dtype=jnp.int32)[None, :]).astype(BF16)


def ranks(expert_ids, expert_count):
    tok_rows, route_count = expert_ids.shape
    flat = expert_ids.reshape(-1)
    hit = flat[:, None] == jnp.arange(expert_count, dtype=jnp.int32)[None, :]
    order = jnp.arange(tok_rows * route_count, dtype=jnp.int32)
    earlier = (order[None, :] < order[:, None]).astype(BF16)
    before = jnp.dot(earlier, hit.astype(BF16), preferred_element_type=F32)
    rank = jnp.sum(jnp.where(hit, before, 0.0), axis=1).astype(jnp.int32)
    return rank.reshape(tok_rows, route_count)


def to_b(a):
    return a.reshape(8, 16, 6, -1).transpose(1, 0, 2, 3).reshape(768, -1)


def to_a(b):
    return b.reshape(16, 8, 6, -1).transpose(1, 0, 2, 3).reshape(768, -1)


def on_device(tokens, expert_ids, gate_num, out_grad, gate_weight, up_weight, down_weight):
    rank = ranks(expert_ids, 64)
    gate = gate_num.astype(F32) / DEN
    rows = jnp.arange(384, dtype=jnp.int32)[:, None]
    slot_b = expert_ids * 6 + rank
    wts = sum(jnp.where(rows == slot_b[None, :, k], gate[None, :, k], 0.0) for k in (0, 1))
    slot_a = (expert_ids % 16) * 48 + (expert_ids // 16) * 6 + rank
    rows = jnp.arange(768, dtype=jnp.int32)[:, None]
    placer = [
        sum((rows == slot_a[None, :, k] + h * 24).astype(F32) for k in (0, 1)).astype(BF16)
        for h in (0, 1)
    ]
    half = tokens.shape[1] // 2
    folded = jnp.concatenate([tokens[:, :half], tokens[:, half:]], axis=0)
    xs = jnp.dot(
        jnp.concatenate(placer, axis=1), folded, preferred_element_type=F32).astype(BF16)
    j = jnp.arange(768, dtype=jnp.int32)
    pi = one_hot(j % 96 // 6 * 48 + j // 96 % 2 * 24 + j // 192 * 6 + j % 6, 768)
    home = j // 48 * 6 + j % 6
    source = j % 48 // 6
    spread = jnp.stack([
        one_hot(jnp.where(source == s % 4 * 2 + s // 4, home, -1), 96) for s in range(8)])
    rows_in, grads_in, wbig = call_dispatch(xs, out_grad, wts.astype(BF16), pi, spread)
    gate_block, up_block, down_block = gate_weight[0], up_weight[0], down_weight[0]
    gate_act = jnp.dot(rows_in, gate_block, preferred_element_type=F32)
    up_act = jnp.dot(rows_in, up_block, preferred_element_type=F32)
    sigmoid_gate = jax.nn.sigmoid(gate_act)
    silu_gate = gate_act * sigmoid_gate
    hidden = to_b((silu_gate * up_act).astype(BF16))
    out_b = jnp.dot(hidden, down_block, preferred_element_type=F32).astype(BF16)
    last = (((1,), (1,)), ((), ()))
    first = (((0,), (0,)), ((), ()))
    hidden_grad = to_a(lax.dot_general(grads_in, down_block, last, preferred_element_type=F32))
    up_grad_act = (hidden_grad * silu_gate).astype(BF16)
    gate_grad_act = (
        hidden_grad * up_act * sigmoid_gate * (1.0 + gate_act * (1.0 - sigmoid_gate))
    ).astype(BF16)
    row_part = lax.dot_general(gate_grad_act, gate_block, last, preferred_element_type=F32)
    row_part = row_part + lax.dot_general(
        up_grad_act, up_block, last, preferred_element_type=F32
    )
    moe_out, token_grad = call_homeward(
        out_b, row_part.astype(BF16), wbig.T, pi.T, jnp.stack([p.T for p in placer]))
    down_grad = lax.dot_general(hidden, grads_in, first, preferred_element_type=F32)
    gate_grad = lax.dot_general(rows_in, gate_grad_act, first, preferred_element_type=F32)
    up_grad = lax.dot_general(rows_in, up_grad_act, first, preferred_element_type=F32)
    return (
        moe_out,
        token_grad,
        gate_grad.astype(BF16)[None],
        up_grad.astype(BF16)[None],
        down_grad.astype(BF16)[None],
    )


def solution(mesh):
    rows = P(("dp", "expert"), None)
    blocks = P(("dp", "expert"), None, None)
    return jax.shard_map(
        on_device,
        mesh=mesh,
        in_specs=(rows, rows, rows, rows, blocks, blocks, blocks),
        out_specs=(rows, rows, blocks, blocks, blocks),
        check_vma=False,
    )
```

```python
import jax
import jax.numpy as jnp
from jax import lax
from jax.experimental import pallas as pl
from jax.experimental.pallas import tpu as pltpu
from jax.sharding import PartitionSpec as P

DEN = 256
MESH = pl.DeviceIdType.MESH
BF16, F32 = jnp.bfloat16, jnp.float32
CHUNKS = 2
PLANE = ((0, 1), (1, 0), (0, 3), (3, 0), (2, 2), (1, 1), (3, 3), (1, 3), (3, 1), (0, 2), (2, 0),
         (1, 2), (3, 2), (2, 1), (2, 3))
DPS = ((1, 0), (3, 0), (2, 0), (1, 1), (3, 1), (2, 1), (0, 1))


def place():
    dp, ex = lax.axis_index("dp"), lax.axis_index("expert")
    return dp // 2, dp % 2, ex // 4, ex % 4


def span(start, size):
    return pl.ds(pl.multiple_of(start, 16), size)


def remote(src, dst, s, r, yy, cc, xx, zz):
    return pltpu.make_async_remote_copy(
        src_ref=src, dst_ref=dst, send_sem=s, recv_sem=r,
        device_id=(yy * 2 + cc, xx * 4 + zz), device_id_type=MESH)


def dispatch(xs, og, wts, pi, spread, x_out, g_out, wbig, a1r, a2s, ogr, wr, b2s, a1_s, a1_r,
             b1_s, b1_r, sb_s, sb_r, w_s, w_r, a2_s, a2_r, b2_s, b2_r, l_s):
    y, c, x, z = place()
    dp, ex = y * 2 + c, x * 4 + z
    half = og.shape[1] // 2
    fold = half // CHUNKS
    wide = og.shape[1] // CHUNKS
    me = c * 4 + y
    own = [
        pltpu.make_async_copy(xs.at[span(ex * 48, 48)], a1r.at[span(ex * 48, 48)], l_s.at[0]),
        pltpu.make_async_copy(og, ogr.at[span(me * 128, 128)], l_s.at[1]),
        pltpu.make_async_copy(wts.at[span(dp % 4 * 96, 96)], wr.at[me], l_s.at[2]),
    ]
    for o in own:
        o.start()
    w_cp = []
    for d, dc in DPS:
        yy, cc = (y + d) % 4, (c + dc) % 2
        w_cp.append(remote(wts.at[span((yy * 2 + cc) % 4 * 96, 96)], wr.at[me],
                           w_s.at[d * 2 + dc], w_r.at[d * 2 + dc], yy, cc, x, z))
        w_cp[-1].start()
    a1, b1, sb, a2, b2, last = [], [], [], [], [], []
    for k in range(CHUNKS):
        thin, cols = pl.ds(k * fold, fold), pl.ds(k * wide, wide)
        b1.append([remote(og.at[:, cols], ogr.at[span(me * 128, 128), cols],
                          b1_s.at[k, d], b1_r.at[k, d], (y + d) % 4, c, x, z) for d in (1, 3, 2)])
        sb.append([remote(og.at[:, cols], ogr.at[span(me * 128, 128), cols],
                          sb_s.at[k, 0], sb_r.at[k, 0], y, 1 - c, x, z)])
        a1.append([])
        for dx, dz in PLANE:
            xx, zz = (x + dx) % 4, (z + dz) % 4
            a1[k].append(remote(
                xs.at[span((xx * 4 + zz) * 48, 48), thin], a1r.at[span(ex * 48, 48), thin],
                a1_s.at[k, dx * 4 + dz], a1_r.at[k, dx * 4 + dz], y, c, xx, zz))
        for cp in b1[k] + sb[k] + a1[k]:
            cp.start()
    for o in own:
        o.wait()
    for w in w_cp:
        w.wait_recv()
    for s in range(8):
        wbig[:, s * 128:(s + 1) * 128] = jnp.dot(
            spread[s], wr[s], preferred_element_type=F32).astype(BF16)
    for k in range(CHUNKS):
        thin, cols = pl.ds(k * fold, fold), pl.ds(k * wide, wide)
        for d, cp in zip((1, 3, 2), b1[k]):
            cp.wait_recv()
            block = ogr.at[span((c * 4 + (y + 4 - d) % 4) * 128, 128), cols]
            sb[k].append(remote(block, block, sb_s.at[k, d], sb_r.at[k, d], y, 1 - c, x, z))
            sb[k][-1].start()
        for cp in a1[k]:
            cp.wait_recv()
        a2.append([])
        for dy in (1, 0):
            for dc in (0, 1):
                cc = (c + dc) % 2
                q = ((y + dy) % 2) * 2 + cc
                for h in range(2):
                    part = pl.ds(h * half + k * fold, fold)
                    a2s[span(q * 96, 96), part] = jnp.dot(
                        pi[span((q * 2 + h) * 96, 96), :], a1r[:, thin],
                        preferred_element_type=F32).astype(BF16)
                    for far in (0, 2):
                        d = dy + far
                        spot = x_out.at[span(dp * 96, 96), part]
                        if d == 0 and dc == 0:
                            cp = pltpu.make_async_copy(
                                a2s.at[span(q * 96, 96), part], spot, l_s.at[3 + k * 2 + h])
                            last.append(cp)
                        else:
                            n = (d * 2 + dc) * 2 + h
                            cp = remote(a2s.at[span(q * 96, 96), part], spot, a2_s.at[k, n],
                                        a2_r.at[k, n], (y + d) % 4, cc, x, z)
                            a2[k].append(cp)
                        cp.start()
        for cp in sb[k]:
            cp.wait_recv()
        for h in range(4):
            band = pl.ds(h * 192, 192)
            b2s[band, cols] = jnp.dot(
                wbig[band, :], ogr[:, cols], preferred_element_type=F32).astype(BF16)
        b2.append([])
        spot = g_out.at[span(ex * 48, 48), cols]
        for dx, dz in PLANE:
            xx, zz = (x + dx) % 4, (z + dz) % 4
            n = dx * 4 + dz
            b2[k].append(remote(b2s.at[span((xx * 4 + zz) * 48, 48), cols], spot,
                                b2_s.at[k, n], b2_r.at[k, n], y, c, xx, zz))
            b2[k][-1].start()
        last.append(pltpu.make_async_copy(b2s.at[span(ex * 48, 48), cols], spot, l_s.at[7 + k]))
        last[-1].start()
    for k in range(CHUNKS):
        for cp in a2[k] + b2[k]:
            cp.wait_recv()
    for cp in last:
        cp.wait()
    for cp in w_cp + sum(a1 + b1 + sb + a2 + b2, []):
        cp.wait_send()


def experts(rows_in, grads_in, gate_w, up_w, down_w, wbig_t, pi_t, placer_t, pab, pba,
            moe, tok, gate_g, up_g, down_g, br, ar, sibr,
            out_b, row_a, partr, backr,
            c1_s, c1_r, d1_s, d1_r, sb_s, sb_r, c2_s, c2_r, d2_s, d2_r, l_s):
    y, c, x, z = place()
    dp, ex = y * 2 + c, x * 4 + z
    half = out_b.shape[1] // 2
    fold = half // CHUNKS
    wide = out_b.shape[1] // CHUNKS
    last = (((1,), (1,)), ((), ()))
    first = (((0,), (0,)), ((), ()))

    def c1_copies(k, dx):
        cols, xx = pl.ds(k * wide, wide), (x + dx) % 4
        made = []
        for dz in (1, 3, 2, 0):
            zz = (z + dz) % 4
            n = dx * 4 + dz
            if n:
                made.append(remote(
                    out_b.at[span((xx * 4 + zz) * 48, 48), cols], br.at[span(ex * 48, 48), cols],
                    c1_s.at[k, n], c1_r.at[k, n], y, c, xx, zz))
        return made

    def d1_copies(k, h):
        piece = pl.ds(h * half + k * fold, fold)
        made = []
        for d, dc in DPS:
            yy, cc = (y + d) % 4, (c + dc) % 2
            n = (d * 2 + dc) * 2 + h
            made.append(remote(
                row_a.at[span((yy * 2 + cc) * 96, 96), piece], ar.at[span(dp * 96, 96), piece],
                d1_s.at[k, n], d1_r.at[k, n], yy, cc, x, z))
        return made

    def own_out(k):
        cols = pl.ds(k * wide, wide)
        return pltpu.make_async_copy(
            out_b.at[span(ex * 48, 48), cols], br.at[span(ex * 48, 48), cols], l_s.at[k])

    def own_row(k, h):
        piece = pl.ds(h * half + k * fold, fold)
        return pltpu.make_async_copy(
            row_a.at[span(dp * 96, 96), piece], ar.at[span(dp * 96, 96), piece],
            l_s.at[2 + k * 2 + h])

    def compute(xv, gv, wg, wu, wd, ga, ua, hid_a, hid_b, hg, gu, in_s):
        loads = [pltpu.make_async_copy(s, t, in_s.at[n]) for n, (s, t) in enumerate((
            (gate_w, wg), (rows_in, xv), (up_w, wu), (down_w, wd), (grads_in, gv)))]
        for cp in loads:
            cp.start()
        for cp in loads[:3]:
            cp.wait()

        @pl.loop(0, 2)
        def _(i):
            band = pl.ds(pl.multiple_of(i * 384, 384), 384)
            ga[band, :] = jnp.dot(xv[band, :], wg[...], preferred_element_type=F32)
            ua[band, :] = jnp.dot(xv[band, :], wu[...], preferred_element_type=F32)
            g = ga[band, :]
            hid_a[band, :] = (g * jax.nn.sigmoid(g) * ua[band, :]).astype(BF16)

        hid_b[...] = jnp.dot(pab[...], hid_a[...], preferred_element_type=F32).astype(BF16)
        loads[3].wait()
        for k in range(CHUNKS):
            cols = pl.ds(k * wide, wide)
            for dx in (1, 3, 2, 0):
                band = span((x + dx) % 4 * 192, 192)
                out_b[band, cols] = jnp.dot(
                    hid_b[band, :], wd[:, cols], preferred_element_type=F32).astype(BF16)
                for cp in c1_copies(k, dx):
                    cp.start()
            own_out(k).start()
        loads[4].wait()

        @pl.loop(0, 2)
        def _(i):
            band = pl.ds(pl.multiple_of(i * 384, 384), 384)
            hg[band, :] = lax.dot_general(gv[band, :], wd[...], last, preferred_element_type=F32)

        high = hg[...].astype(BF16)
        low = (hg[...] - high.astype(F32)).astype(BF16)
        hg[...] = (jnp.dot(pba[...], high, preferred_element_type=F32)
                   + jnp.dot(pba[...], low, preferred_element_type=F32))

        @pl.loop(0, 4)
        def _(i):
            band = pl.ds(pl.multiple_of(i * 192, 192), 192)
            g, h = ga[band, :], hg[band, :]
            sg = jax.nn.sigmoid(g)
            gu[band, 0:384] = (h * ua[band, :] * sg * (1.0 + g * (1.0 - sg))).astype(BF16)
            gu[band, 384:768] = (h * (g * sg)).astype(BF16)

        for k in range(CHUNKS):
            for h in range(2):
                piece = pl.ds(h * half + k * fold, fold)

                @pl.loop(0, 2)
                def _(i):
                    band = pl.ds(pl.multiple_of(i * 384, 384), 384)
                    row_a[band, piece] = (
                        lax.dot_general(gu[band, 0:384], wg[piece, :], last,
                                        preferred_element_type=F32)
                        + lax.dot_general(gu[band, 384:768], wu[piece, :], last,
                                          preferred_element_type=F32)).astype(BF16)

                for cp in d1_copies(k, h):
                    cp.start()
                own_row(k, h).start()

        @pl.loop(0, 8)
        def _(i):
            cols = pl.ds(pl.multiple_of(i * 512, 512), 512)
            wd[:, cols] = lax.dot_general(
                hid_b[...], gv[:, cols], first, preferred_element_type=F32).astype(BF16)

        @pl.loop(0, 16)
        def _(i):
            cols = pl.ds(pl.multiple_of(i * 256, 256), 256)
            both = lax.dot_general(
                xv[:, cols], gu[...], first, preferred_element_type=F32).astype(BF16)
            wg[cols, :] = both[:, 0:384]
            wu[cols, :] = both[:, 384:768]

        saves = [pltpu.make_async_copy(s, t, in_s.at[5 + n]) for n, (s, t) in enumerate((
            (wg, gate_g), (wu, up_g), (wd, down_g)))]
        for cp in saves:
            cp.start()
        for cp in saves:
            cp.wait()

    w = out_b.shape[1]
    pl.run_scoped(
        compute, vm(768, w), vm(768, w), vm(w, 384), vm(w, 384), vm(384, w),
        pltpu.VMEM((768, 384), F32), pltpu.VMEM((768, 384), F32), vm(768, 384), vm(768, 384),
        pltpu.VMEM((768, 384), F32), vm(768, 768), pltpu.SemaphoreType.DMA((8,)))

    def combine(brl, arl, tot, part, sibl, summed, back, in_s):
        c1 = [sum((c1_copies(k, dx) for dx in range(4)), []) for k in range(CHUNKS)]
        d1 = [d1_copies(k, 0) + d1_copies(k, 1) for k in range(CHUNKS)]
        sb, c2, d2, own2 = [], [], [], []
        for k in range(CHUNKS):
            thin, cols = pl.ds(k * fold, fold), pl.ds(k * wide, wide)
            for cp in (own_out(k), own_row(k, 0), own_row(k, 1)):
                cp.wait()
            for cp in c1[k]:
                cp.wait_recv()
            load = pltpu.make_async_copy(br.at[:, cols], brl, in_s.at[0])
            load.start()
            load.wait()
            for s in range(4):
                band = pl.ds(s * 256, 256)
                part[band, cols] = jnp.dot(
                    wbig_t[band, :], brl[...], preferred_element_type=F32).astype(BF16)
            sb.append(remote(part.at[span((1 - c) * 512, 512), cols], sibr.at[:, cols],
                             sb_s.at[k], sb_r.at[k], y, 1 - c, x, z))
            sb[k].start()
            for cp in d1[k]:
                cp.wait_recv()
            more = [pltpu.make_async_copy(
                ar.at[:, pl.ds(h * half + k * fold, fold)], arl.at[h], in_s.at[1 + h])
                for h in range(2)]
            for cp in more:
                cp.start()
            for cp in more:
                cp.wait()
            for q in range(4):
                for h in range(2):
                    tot[(q * 2 + h) * 96:(q * 2 + h + 1) * 96, :] = (
                        arl[h, q * 96:(q + 1) * 96, :].astype(F32)
                        + arl[h, 384 + q * 96:384 + (q + 1) * 96, :].astype(F32)).astype(BF16)
            for h in range(4):
                band = pl.ds(h * 192, 192)
                back[band, thin] = jnp.dot(
                    pi_t[band, :], tot[...], preferred_element_type=F32).astype(BF16)
            d2.append([])
            for dx, dz in PLANE:
                xx, zz = (x + dx) % 4, (z + dz) % 4
                n = dx * 4 + dz
                d2[k].append(remote(
                    back.at[span((xx * 4 + zz) * 48, 48), thin],
                    backr.at[span(ex * 48, 48), thin],
                    d2_s.at[k, n], d2_r.at[k, n], y, c, xx, zz))
            own2.append([pltpu.make_async_copy(
                back.at[span(ex * 48, 48), thin], backr.at[span(ex * 48, 48), thin],
                l_s.at[6 + k])])
            for cp in d2[k] + own2[k]:
                cp.start()
            sb[k].wait_recv()
            load = pltpu.make_async_copy(sibr.at[:, cols], sibl, in_s.at[3])
            load.start()
            load.wait()
            summed[:, cols] = (part[span(c * 512, 512), cols].astype(F32)
                               + sibl[...].astype(F32)).astype(BF16)
            c2.append([])
            spot = partr.at[span(y * 128, 128), cols]
            for d in (1, 3, 2):
                yy = (y + d) % 4
                c2[k].append(remote(summed.at[span(yy * 128, 128), cols], spot,
                                    c2_s.at[k, d], c2_r.at[k, d], yy, c, x, z))
                c2[k][-1].start()
            own2[k].append(pltpu.make_async_copy(summed.at[span(y * 128, 128), cols], spot,
                                                 l_s.at[8 + k]))
            own2[k][-1].start()
        for k in range(CHUNKS):
            thin, cols = pl.ds(k * fold, fold), pl.ds(k * wide, wide)
            for cp in own2[k]:
                cp.wait()
            for cp in c2[k] + d2[k]:
                cp.wait_recv()
            for h in range(2):
                tok[:, pl.ds(h * half + k * fold, fold)] = jnp.dot(
                    placer_t[h], backr[:, thin], preferred_element_type=F32).astype(BF16)
            moe[:, cols] = sum(
                partr[s * 128:(s + 1) * 128, cols].astype(F32) for s in range(4)).astype(BF16)
        for cp in sum(c1 + d1 + c2 + d2, sb):
            cp.wait_send()

    pl.run_scoped(
        combine, vm(768, wide), vm(2, 768, fold), vm(768, fold), vm(1024, w), vm(512, wide),
        vm(512, w), vm(768, half), pltpu.SemaphoreType.DMA((4,)))


VM = pl.BlockSpec(memory_space=pltpu.VMEM)
HB = pl.BlockSpec(memory_space=pltpu.HBM)


def sems(*sizes):
    return [pltpu.SemaphoreType.DMA(s) for s in sizes for _ in (0, 1)]


def vm(*shape):
    return pltpu.VMEM(shape, BF16)


def out(*shape):
    return jax.ShapeDtypeStruct(shape, BF16)


def call_dispatch(xs, og, wts, pi, spread):
    w, k = og.shape[1], CHUNKS
    return pl.pallas_call(
        dispatch,
        out_shape=(out(768, w), out(768, w), out(768, 1024)),
        in_specs=[VM] * 5,
        out_specs=(HB, HB, VM),
        scratch_shapes=[
            vm(768, w // 2), vm(384, w), vm(1024, w), vm(8, 96, 128), vm(768, w),
            *sems((k, 16), (k, 4), (k, 4), (8,), (k, 16), (k, 16)),
            pltpu.SemaphoreType.DMA((9,))],
        compiler_params=pltpu.CompilerParams(has_side_effects=True, vmem_limit_bytes=56 << 20),
    )(xs, og, wts, pi, spread)


def call_experts(*args):
    w, k = args[0].shape[1], CHUNKS
    return pl.pallas_call(
        experts,
        out_shape=(out(128, w), out(128, w), out(w, 384), out(w, 384), out(384, w),
                   out(768, w), out(768, w), out(512, w)),
        in_specs=[HB] * 5 + [VM] * 5,
        out_specs=(VM, VM) + (HB,) * 6,
        scratch_shapes=[
            vm(768, w), vm(768, w), vm(512, w), vm(768, w // 2),
            *sems((k, 16), (k, 16), (k,), (k, 4), (k, 16)), pltpu.SemaphoreType.DMA((10,))],
        compiler_params=pltpu.CompilerParams(has_side_effects=True, vmem_limit_bytes=60 << 20),
    )(*args)


def one_hot(index, size):
    return (index[:, None] == jnp.arange(size, dtype=jnp.int32)[None, :]).astype(BF16)


def ranks(expert_ids, expert_count):
    tok_rows, route_count = expert_ids.shape
    flat = expert_ids.reshape(-1)
    hit = flat[:, None] == jnp.arange(expert_count, dtype=jnp.int32)[None, :]
    order = jnp.arange(tok_rows * route_count, dtype=jnp.int32)
    earlier = (order[None, :] < order[:, None]).astype(BF16)
    before = jnp.dot(earlier, hit.astype(BF16), preferred_element_type=F32)
    rank = jnp.sum(jnp.where(hit, before, 0.0), axis=1).astype(jnp.int32)
    return rank.reshape(tok_rows, route_count)


def on_device(tokens, expert_ids, gate_num, out_grad, gate_weight, up_weight, down_weight):
    rank = ranks(expert_ids, 64)
    gate = gate_num.astype(F32) / DEN
    rows = jnp.arange(384, dtype=jnp.int32)[:, None]
    slot_b = expert_ids * 6 + rank
    wts = sum(jnp.where(rows == slot_b[None, :, k], gate[None, :, k], 0.0) for k in (0, 1))
    slot_a = (expert_ids % 16) * 48 + (expert_ids // 16) * 6 + rank
    rows = jnp.arange(768, dtype=jnp.int32)[:, None]
    placer = [
        sum((rows == slot_a[None, :, k] + h * 24).astype(F32) for k in (0, 1)).astype(BF16)
        for h in (0, 1)
    ]
    half = tokens.shape[1] // 2
    folded = jnp.concatenate([tokens[:, :half], tokens[:, half:]], axis=0)
    xs = jnp.dot(
        jnp.concatenate(placer, axis=1), folded, preferred_element_type=F32).astype(BF16)
    j = jnp.arange(768, dtype=jnp.int32)
    pi = one_hot(j % 96 // 6 * 48 + j // 96 % 2 * 24 + j // 192 * 6 + j % 6, 768)
    home = j // 48 * 6 + j % 6
    source = j % 48 // 6
    spread = jnp.stack([
        one_hot(jnp.where(source == s % 4 * 2 + s // 4, home, -1), 96) for s in range(8)])
    rows_in, grads_in, wbig = call_dispatch(xs, out_grad, wts.astype(BF16), pi, spread)
    order = j % 48 // 6 * 96 + j // 48 * 6 + j % 6
    pab = one_hot(order, 768)
    back = j % 96 // 6 * 48 + j // 96 * 6 + j % 6
    pba = one_hot(back, 768)
    moe_out, token_grad, gate_grad, up_grad, down_grad, *_ = call_experts(
        rows_in, grads_in, gate_weight[0], up_weight[0], down_weight[0], wbig.T, pi.T,
        jnp.stack([p.T for p in placer]), pab, pba)
    return moe_out, token_grad, gate_grad[None], up_grad[None], down_grad[None]


def solution(mesh):
    rows = P(("dp", "expert"), None)
    blocks = P(("dp", "expert"), None, None)
    return jax.shard_map(
        on_device,
        mesh=mesh,
        in_specs=(rows, rows, rows, rows, blocks, blocks, blocks),
        out_specs=(rows, rows, blocks, blocks, blocks),
        check_vma=False,
    )
```

```python
import jax
import jax.numpy as jnp
import numpy as np
from jax import lax
from jax.experimental import pallas as pl
from jax.experimental.pallas import tpu as pltpu
from jax.sharding import PartitionSpec as P

DEN = 256
MESH = pl.DeviceIdType.MESH
BF16, F32 = jnp.bfloat16, jnp.float32
CHUNKS = 2
PLANE = ((0, 1), (1, 0), (0, 3), (3, 0), (2, 2), (1, 1), (3, 3), (1, 3), (3, 1), (0, 2), (2, 0),
         (1, 2), (3, 2), (2, 1), (2, 3))
DPS = ((1, 0), (3, 0), (2, 0), (1, 1), (3, 1), (2, 1), (0, 1))


def place():
    dp, ex = lax.axis_index("dp"), lax.axis_index("expert")
    return dp // 2, dp % 2, ex // 4, ex % 4


def span(start, size):
    return pl.ds(pl.multiple_of(start, 16), size)


def remote(src, dst, s, r, yy, cc, xx, zz):
    return pltpu.make_async_remote_copy(
        src_ref=src, dst_ref=dst, send_sem=s, recv_sem=r,
        device_id=(yy * 2 + cc, xx * 4 + zz), device_id_type=MESH)


def dispatch(xs, og, wts, pi, spread, x_out, g_out, wbig_t, wbig, a1r, a2s, ogr, wr, b2s, a1_s, a1_r,
             b1_s, b1_r, sb_s, sb_r, w_s, w_r, a2_s, a2_r, b2_s, b2_r, l_s):
    y, c, x, z = place()
    dp, ex = y * 2 + c, x * 4 + z
    half = og.shape[1] // 2
    fold = half // CHUNKS
    wide = og.shape[1] // CHUNKS
    me = c * 4 + y
    own = [
        pltpu.make_async_copy(xs.at[span(ex * 48, 48)], a1r.at[span(ex * 48, 48)], l_s.at[0]),
        pltpu.make_async_copy(og, ogr.at[span(me * 128, 128)], l_s.at[1]),
        pltpu.make_async_copy(wts.at[span(dp % 4 * 96, 96)], wr.at[me], l_s.at[2]),
    ]
    for o in own:
        o.start()
    w_cp = []
    for d, dc in DPS:
        yy, cc = (y + d) % 4, (c + dc) % 2
        w_cp.append(remote(wts.at[span((yy * 2 + cc) % 4 * 96, 96)], wr.at[me],
                           w_s.at[d * 2 + dc], w_r.at[d * 2 + dc], yy, cc, x, z))
        w_cp[-1].start()
    a1, b1, sb, a2, b2, last = [], [], [], [], [], []
    for k in range(CHUNKS):
        thin, cols = pl.ds(k * fold, fold), pl.ds(k * wide, wide)
        b1.append([remote(og.at[:, cols], ogr.at[span(me * 128, 128), cols],
                          b1_s.at[k, d], b1_r.at[k, d], (y + d) % 4, c, x, z) for d in (1, 3, 2)])
        sb.append([remote(og.at[:, cols], ogr.at[span(me * 128, 128), cols],
                          sb_s.at[k, 0], sb_r.at[k, 0], y, 1 - c, x, z)])
        a1.append([])
        for dx, dz in PLANE:
            xx, zz = (x + dx) % 4, (z + dz) % 4
            a1[k].append(remote(
                xs.at[span((xx * 4 + zz) * 48, 48), thin], a1r.at[span(ex * 48, 48), thin],
                a1_s.at[k, dx * 4 + dz], a1_r.at[k, dx * 4 + dz], y, c, xx, zz))
        for cp in b1[k] + sb[k] + a1[k]:
            cp.start()
    for o in own:
        o.wait()
    for w in w_cp:
        w.wait_recv()
    for s in range(8):
        wbig[:, s * 128:(s + 1) * 128] = jnp.dot(
            spread[s], wr[s], preferred_element_type=F32).astype(BF16)
        wbig_t[s * 128:(s + 1) * 128, :] = lax.dot_general(
            wr[s], spread[s], (((0,), (1,)), ((), ())), preferred_element_type=F32).astype(BF16)
    for k in range(CHUNKS):
        thin, cols = pl.ds(k * fold, fold), pl.ds(k * wide, wide)
        for d, cp in zip((1, 3, 2), b1[k]):
            cp.wait_recv()
            block = ogr.at[span((c * 4 + (y + 4 - d) % 4) * 128, 128), cols]
            sb[k].append(remote(block, block, sb_s.at[k, d], sb_r.at[k, d], y, 1 - c, x, z))
            sb[k][-1].start()
        for cp in a1[k]:
            cp.wait_recv()
        a2.append([])
        for dy in (1, 0):
            for dc in (0, 1):
                cc = (c + dc) % 2
                q = ((y + dy) % 2) * 2 + cc
                for h in range(2):
                    part = pl.ds(h * half + k * fold, fold)
                    a2s[span(q * 96, 96), part] = jnp.dot(
                        pi[span((q * 2 + h) * 96, 96), :], a1r[:, thin],
                        preferred_element_type=F32).astype(BF16)
                    for far in (0, 2):
                        d = dy + far
                        spot = x_out.at[span(dp * 96, 96), part]
                        if d == 0 and dc == 0:
                            cp = pltpu.make_async_copy(
                                a2s.at[span(q * 96, 96), part], spot, l_s.at[3 + k * 2 + h])
                            last.append(cp)
                        else:
                            n = (d * 2 + dc) * 2 + h
                            cp = remote(a2s.at[span(q * 96, 96), part], spot, a2_s.at[k, n],
                                        a2_r.at[k, n], (y + d) % 4, cc, x, z)
                            a2[k].append(cp)
                        cp.start()
        for cp in sb[k]:
            cp.wait_recv()
        for h in range(4):
            band = pl.ds(h * 192, 192)
            b2s[band, cols] = jnp.dot(
                wbig[band, :], ogr[:, cols], preferred_element_type=F32).astype(BF16)
        b2.append([])
        spot = g_out.at[span(ex * 48, 48), cols]
        for dx, dz in PLANE:
            xx, zz = (x + dx) % 4, (z + dz) % 4
            n = dx * 4 + dz
            b2[k].append(remote(b2s.at[span((xx * 4 + zz) * 48, 48), cols], spot,
                                b2_s.at[k, n], b2_r.at[k, n], y, c, xx, zz))
            b2[k][-1].start()
        last.append(pltpu.make_async_copy(b2s.at[span(ex * 48, 48), cols], spot,
                                          l_s.at[3 + 2 * CHUNKS + k]))
        last[-1].start()
    for k in range(CHUNKS):
        for cp in a2[k] + b2[k]:
            cp.wait_recv()
    for cp in last:
        cp.wait()
    for cp in w_cp + sum(a1 + b1 + sb + a2 + b2, []):
        cp.wait_send()


def experts(rows_in, grads_in, gate_w, up_w, down_w, wbig_t, pi_t, placer_t, pab, pba,
            moe, tok, gate_g, up_g, down_g, br, ar, sibr,
            out_b, row_a, partr, backr,
            c1_s, c1_r, d1_s, d1_r, sb_s, sb_r, c2_s, c2_r, d2_s, d2_r, l_s):
    y, c, x, z = place()
    dp, ex = y * 2 + c, x * 4 + z
    half = out_b.shape[1] // 2
    fold = half // CHUNKS
    wide = out_b.shape[1] // CHUNKS
    last = (((1,), (1,)), ((), ()))
    first = (((0,), (0,)), ((), ()))

    def c1_copies(k, dx):
        cols, xx = pl.ds(k * wide, wide), (x + dx) % 4
        made = []
        for dz in (1, 3, 2, 0):
            zz = (z + dz) % 4
            n = dx * 4 + dz
            if n:
                made.append(remote(
                    out_b.at[span((xx * 4 + zz) * 48, 48), cols], br.at[span(ex * 48, 48), cols],
                    c1_s.at[k, n], c1_r.at[k, n], y, c, xx, zz))
        return made

    def d1_copies(k, h):
        piece = pl.ds(h * half + k * fold, fold)
        made = []
        for d, dc in DPS:
            yy, cc = (y + d) % 4, (c + dc) % 2
            n = (d * 2 + dc) * 2 + h
            made.append(remote(
                row_a.at[span((yy * 2 + cc) * 96, 96), piece], ar.at[span(dp * 96, 96), piece],
                d1_s.at[k, n], d1_r.at[k, n], yy, cc, x, z))
        return made

    def own_out(k):
        cols = pl.ds(k * wide, wide)
        return pltpu.make_async_copy(
            out_b.at[span(ex * 48, 48), cols], br.at[span(ex * 48, 48), cols], l_s.at[k])

    def own_row(k, h):
        piece = pl.ds(h * half + k * fold, fold)
        return pltpu.make_async_copy(
            row_a.at[span(dp * 96, 96), piece], ar.at[span(dp * 96, 96), piece],
            l_s.at[CHUNKS + k * 2 + h])

    def compute(xv, gv, wg, wu, wd, ga, ua, hid_a, hid_b, hg, gu, in_s):
        loads = [pltpu.make_async_copy(s, t, in_s.at[n]) for n, (s, t) in enumerate((
            (gate_w, wg), (rows_in, xv), (up_w, wu), (down_w, wd), (grads_in, gv)))]
        for cp in loads:
            cp.start()
        for cp in loads[:3]:
            cp.wait()

        @pl.loop(0, 2)
        def _(i):
            band = pl.ds(pl.multiple_of(i * 384, 384), 384)
            ga[band, :] = jnp.dot(xv[band, :], wg[...], preferred_element_type=F32)
            ua[band, :] = jnp.dot(xv[band, :], wu[...], preferred_element_type=F32)
            g = ga[band, :]
            hid_a[band, :] = (g * jax.nn.sigmoid(g) * ua[band, :]).astype(BF16)

        hid_b[...] = jnp.dot(pab[...], hid_a[...], preferred_element_type=F32).astype(BF16)
        loads[3].wait()
        for k in range(CHUNKS):
            cols = pl.ds(k * wide, wide)
            for dx in (1, 3, 2, 0):
                band = span((x + dx) % 4 * 192, 192)
                out_b[band, cols] = jnp.dot(
                    hid_b[band, :], wd[:, cols], preferred_element_type=F32).astype(BF16)
                for cp in c1_copies(k, dx):
                    cp.start()
            own_out(k).start()
        loads[4].wait()

        @pl.loop(0, 2)
        def _(i):
            band = pl.ds(pl.multiple_of(i * 384, 384), 384)
            hg[band, :] = lax.dot_general(gv[band, :], wd[...], last, preferred_element_type=F32)

        high = hg[...].astype(BF16)
        low = (hg[...] - high.astype(F32)).astype(BF16)
        hg[...] = (jnp.dot(pba[...], high, preferred_element_type=F32)
                   + jnp.dot(pba[...], low, preferred_element_type=F32))

        @pl.loop(0, 4)
        def _(i):
            band = pl.ds(pl.multiple_of(i * 192, 192), 192)
            g, h = ga[band, :], hg[band, :]
            sg = jax.nn.sigmoid(g)
            gu[band, 0:384] = (h * ua[band, :] * sg * (1.0 + g * (1.0 - sg))).astype(BF16)
            gu[band, 384:768] = (h * (g * sg)).astype(BF16)

        for k in range(CHUNKS):
            for h in range(2):
                piece = pl.ds(h * half + k * fold, fold)

                @pl.loop(0, 2)
                def _(i):
                    band = pl.ds(pl.multiple_of(i * 384, 384), 384)
                    row_a[band, piece] = (
                        lax.dot_general(gu[band, 0:384], wg[piece, :], last,
                                        preferred_element_type=F32)
                        + lax.dot_general(gu[band, 384:768], wu[piece, :], last,
                                          preferred_element_type=F32)).astype(BF16)

                for cp in d1_copies(k, h):
                    cp.start()
                own_row(k, h).start()

        @pl.loop(0, 8)
        def _(i):
            cols = pl.ds(pl.multiple_of(i * 512, 512), 512)
            wd[:, cols] = lax.dot_general(
                hid_b[...], gv[:, cols], first, preferred_element_type=F32).astype(BF16)

        @pl.loop(0, 16)
        def _(i):
            cols = pl.ds(pl.multiple_of(i * 256, 256), 256)
            both = lax.dot_general(
                xv[:, cols], gu[...], first, preferred_element_type=F32).astype(BF16)
            wg[cols, :] = both[:, 0:384]
            wu[cols, :] = both[:, 384:768]

        saves = [pltpu.make_async_copy(s, t, in_s.at[5 + n]) for n, (s, t) in enumerate((
            (wg, gate_g), (wu, up_g), (wd, down_g)))]
        for cp in saves:
            cp.start()
        for cp in saves:
            cp.wait()

    w = out_b.shape[1]
    pl.run_scoped(
        compute, vm(768, w), vm(768, w), vm(w, 384), vm(w, 384), vm(384, w),
        pltpu.VMEM((768, 384), F32), pltpu.VMEM((768, 384), F32), vm(768, 384), vm(768, 384),
        pltpu.VMEM((768, 384), F32), vm(768, 768), pltpu.SemaphoreType.DMA((8,)))

    def combine(brl, arl, tot, part, sibl, summed, back, in_s):
        c1 = [sum((c1_copies(k, dx) for dx in range(4)), []) for k in range(CHUNKS)]
        d1 = [d1_copies(k, 0) + d1_copies(k, 1) for k in range(CHUNKS)]
        sb, c2, d2, own2 = [], [], [], []
        for k in range(CHUNKS):
            thin, cols = pl.ds(k * fold, fold), pl.ds(k * wide, wide)
            for cp in (own_out(k), own_row(k, 0), own_row(k, 1)):
                cp.wait()
            for cp in c1[k]:
                cp.wait_recv()
            load = pltpu.make_async_copy(br.at[:, cols], brl, in_s.at[0])
            load.start()
            load.wait()
            for s in range(4):
                band = pl.ds(s * 256, 256)
                part[band, cols] = jnp.dot(
                    wbig_t[band, :], brl[...], preferred_element_type=F32).astype(BF16)
            sb.append(remote(part.at[span((1 - c) * 512, 512), cols], sibr.at[:, cols],
                             sb_s.at[k], sb_r.at[k], y, 1 - c, x, z))
            sb[k].start()
            for cp in d1[k]:
                cp.wait_recv()
            more = [pltpu.make_async_copy(
                ar.at[:, pl.ds(h * half + k * fold, fold)], arl.at[h], in_s.at[1 + h])
                for h in range(2)]
            for cp in more:
                cp.start()
            for cp in more:
                cp.wait()
            for q in range(4):
                for h in range(2):
                    tot[(q * 2 + h) * 96:(q * 2 + h + 1) * 96, :] = (
                        arl[h, q * 96:(q + 1) * 96, :].astype(F32)
                        + arl[h, 384 + q * 96:384 + (q + 1) * 96, :].astype(F32)).astype(BF16)
            for h in range(4):
                band = pl.ds(h * 192, 192)
                back[band, thin] = jnp.dot(
                    pi_t[band, :], tot[...], preferred_element_type=F32).astype(BF16)
            d2.append([])
            for dx, dz in PLANE:
                xx, zz = (x + dx) % 4, (z + dz) % 4
                n = dx * 4 + dz
                d2[k].append(remote(
                    back.at[span((xx * 4 + zz) * 48, 48), thin],
                    backr.at[span(ex * 48, 48), thin],
                    d2_s.at[k, n], d2_r.at[k, n], y, c, xx, zz))
            own2.append([pltpu.make_async_copy(
                back.at[span(ex * 48, 48), thin], backr.at[span(ex * 48, 48), thin],
                l_s.at[3 * CHUNKS + k])])
            for cp in d2[k] + own2[k]:
                cp.start()
            sb[k].wait_recv()
            load = pltpu.make_async_copy(sibr.at[:, cols], sibl, in_s.at[3])
            load.start()
            load.wait()
            summed[:, cols] = (part[span(c * 512, 512), cols].astype(F32)
                               + sibl[...].astype(F32)).astype(BF16)
            c2.append([])
            spot = partr.at[span(y * 128, 128), cols]
            for d in (1, 3, 2):
                yy = (y + d) % 4
                c2[k].append(remote(summed.at[span(yy * 128, 128), cols], spot,
                                    c2_s.at[k, d], c2_r.at[k, d], yy, c, x, z))
                c2[k][-1].start()
            own2[k].append(pltpu.make_async_copy(summed.at[span(y * 128, 128), cols], spot,
                                                 l_s.at[4 * CHUNKS + k]))
            own2[k][-1].start()
        for k in range(CHUNKS):
            thin, cols = pl.ds(k * fold, fold), pl.ds(k * wide, wide)
            for cp in own2[k]:
                cp.wait()
            for cp in c2[k] + d2[k]:
                cp.wait_recv()
            for h in range(2):
                tok[:, pl.ds(h * half + k * fold, fold)] = jnp.dot(
                    placer_t[h], backr[:, thin], preferred_element_type=F32).astype(BF16)
            moe[:, cols] = sum(
                partr[s * 128:(s + 1) * 128, cols].astype(F32) for s in range(4)).astype(BF16)
        for cp in sum(c1 + d1 + c2 + d2, sb):
            cp.wait_send()

    pl.run_scoped(
        combine, vm(768, wide), vm(2, 768, fold), vm(768, fold), vm(1024, w), vm(512, wide),
        vm(512, w), vm(768, half), pltpu.SemaphoreType.DMA((4,)))


VM = pl.BlockSpec(memory_space=pltpu.VMEM)
HB = pl.BlockSpec(memory_space=pltpu.HBM)


def sems(*sizes):
    return [pltpu.SemaphoreType.DMA(s) for s in sizes for _ in (0, 1)]


def vm(*shape):
    return pltpu.VMEM(shape, BF16)


def out(*shape):
    return jax.ShapeDtypeStruct(shape, BF16)


def call_dispatch(xs, og, wts, pi, spread):
    w, k = og.shape[1], CHUNKS
    return pl.pallas_call(
        dispatch,
        out_shape=(out(768, w), out(768, w), out(1024, 768)),
        in_specs=[VM] * 5,
        out_specs=(HB, HB, VM),
        scratch_shapes=[
            vm(768, 1024), vm(768, w // 2), vm(384, w), vm(1024, w), vm(8, 96, 128), vm(768, w),
            *sems((k, 16), (k, 4), (k, 4), (8,), (k, 16), (k, 16)),
            pltpu.SemaphoreType.DMA((3 + 3 * k,))],
        compiler_params=pltpu.CompilerParams(has_side_effects=True, vmem_limit_bytes=56 << 20),
    )(xs, og, wts, pi, spread)


def call_experts(*args):
    w, k = args[0].shape[1], CHUNKS
    return pl.pallas_call(
        experts,
        out_shape=(out(128, w), out(128, w), out(w, 384), out(w, 384), out(384, w),
                   out(768, w), out(768, w), out(512, w)),
        in_specs=[HB] * 5 + [VM] * 5,
        out_specs=(VM, VM) + (HB,) * 6,
        scratch_shapes=[
            vm(768, w), vm(768, w), vm(512, w), vm(768, w // 2),
            *sems((k, 16), (k, 16), (k,), (k, 4), (k, 16)), pltpu.SemaphoreType.DMA((5 * k,))],
        compiler_params=pltpu.CompilerParams(has_side_effects=True, vmem_limit_bytes=60 << 20),
    )(*args)


def one_hot(index, size):
    return (index[:, None] == np.arange(size)[None, :]).astype(jnp.bfloat16)


def orders():
    j = np.arange(768)
    pi = one_hot(j % 96 // 6 * 48 + j // 96 % 2 * 24 + j // 192 * 6 + j % 6, 768)
    pab = one_hot(j % 48 // 6 * 96 + j // 48 * 6 + j % 6, 768)
    home, source = j // 48 * 6 + j % 6, j % 48 // 6
    spread = np.stack([
        one_hot(np.where(source == s % 4 * 2 + s // 4, home, -1), 96) for s in range(8)])
    return pi, pab, spread


def ranks(expert_ids, expert_count):
    tok_rows, route_count = expert_ids.shape
    flat = expert_ids.reshape(-1)
    hit = flat[:, None] == jnp.arange(expert_count, dtype=jnp.int32)[None, :]
    order = jnp.arange(tok_rows * route_count, dtype=jnp.int32)
    earlier = (order[None, :] < order[:, None]).astype(BF16)
    before = jnp.dot(earlier, hit.astype(BF16), preferred_element_type=F32)
    rank = jnp.sum(jnp.where(hit, before, 0.0), axis=1).astype(jnp.int32)
    return rank.reshape(tok_rows, route_count)


def on_device(tokens, expert_ids, gate_num, out_grad, gate_weight, up_weight, down_weight):
    rank = ranks(expert_ids, 64)
    gate = gate_num.astype(F32) / DEN
    rows = jnp.arange(384, dtype=jnp.int32)[:, None]
    slot_b = expert_ids * 6 + rank
    wts = sum(jnp.where(rows == slot_b[None, :, k], gate[None, :, k], 0.0) for k in (0, 1))
    slot_a = (expert_ids % 16) * 48 + (expert_ids // 16) * 6 + rank
    rows = jnp.arange(768, dtype=jnp.int32)
    hit = [
        sum((rows[:, None] == slot_a[None, :, k] + h * 24).astype(F32) for k in (0, 1))
        for h in (0, 1)
    ]
    placer = jnp.concatenate(hit, axis=1).astype(BF16)
    placer_t = jnp.stack([
        sum((rows[None, :] == slot_a[:, k, None] + h * 24).astype(F32) for k in (0, 1))
        for h in (0, 1)
    ]).astype(BF16)
    half = tokens.shape[1] // 2
    folded = jnp.concatenate([tokens[:, :half], tokens[:, half:]], axis=0)
    xs = jnp.dot(placer, folded, preferred_element_type=F32).astype(BF16)
    pi, pab, spread = orders()
    rows_in, grads_in, wbig_t = call_dispatch(xs, out_grad, wts.astype(BF16), pi, spread)
    moe_out, token_grad, gate_grad, up_grad, down_grad, *_ = call_experts(
        rows_in, grads_in, gate_weight[0], up_weight[0], down_weight[0], wbig_t, pi.T, placer_t,
        pab, pab.T)
    return moe_out, token_grad, gate_grad[None], up_grad[None], down_grad[None]


def solution(mesh):
    rows = P(("dp", "expert"), None)
    blocks = P(("dp", "expert"), None, None)
    return jax.shard_map(
        on_device,
        mesh=mesh,
        in_specs=(rows, rows, rows, rows, blocks, blocks, blocks),
        out_specs=(rows, rows, blocks, blocks, blocks),
        check_vma=False,
    )
```
